32 devices in a mesh: tile: 8 (over y, x, core), frame: 4 (over z).
Axes of the slice: x: 2, y: 2, z: 4, core: 2. Of those that a mesh axis runs over, the one named last changes fastest.
Arguments:
- video: float32 [16, 16, 160, 128], P('frame', 'tile'), may hold values from -6 to 6
- norm_gain: float32 [2, 2, 128], replicated, may hold values from 0.1 to 1.9
- space_weight: float32 [2, 3, 3, 128, 128], replicated, may hold values from -0.1875 to 0.1875
- time_weight: float32 [2, 3, 128, 128], replicated, may hold values from -0.3125 to 0.3125
- down_weight: float32 [3, 3, 128, 256], replicated, may hold values from -0.1875 to 0.1875
- attn_gain: float32 [256], replicated, may hold values from 0.1 to 1.9
- w_query: float32 [256, 256], replicated, may hold values from -4 to 4
- w_key: float32 [256, 256], replicated, may hold values from -4 to 4
- w_value: float32 [256, 256], replicated, may hold values from -0.375 to 0.375
- w_out: float32 [256, 256], replicated, may hold values from -0.375 to 0.375
Outputs:
- encoded: float32 [32, 320, 256], P(('frame', 'tile'))
The draws below stay inside these ranges and needn't reach their ends.
All inputs are finite; a program needn't handle non-finite values.
Results may differ from the reference program's by a relative error of at most 0.0003.
Values sent between devices are 32-bit elements; how exact they have to be, the bound alone decides.
No kernel may reach another device: no remote copies, remote signals or barrier semaphores. Data moves between devices by JAX's collectives and lax.ppermute only.
A program may use at most 64 MiB of HBM per device.

```python
import jax
import jax.numpy as jnp
from jax import lax

C = 128
C2 = 256
W = 160
FRAMES = 16
H = 16
GROUP = 2
PT = 40
ATOK = 320
KEYS = 640
FBLOCKS = 32
N_TILE = 8


def draw_w_query(key, part):
    base = jax.random.normal(jax.random.fold_in(key, 11), (C2, C2), jnp.float32)
    base = jnp.clip(base, -4.0, 4.0) * C2 ** (-0.5)
    return base


def draw_w_key(key, part):
    base = jax.random.normal(jax.random.fold_in(key, 12), (C2, C2), jnp.float32)
    base = jnp.clip(base, -4.0, 4.0) * C2 ** (-0.5)
    return base


def block_levels(own_key, extent, split, low, top_value):
    level, own = 1.0, jax.random.fold_in(own_key, 6)
    for axis_at, blocks in split:
        steps = jnp.exp(jax.random.uniform(jax.random.fold_in(own, axis_at), (blocks,), jnp.float32, low / len(split), top_value / len(split)))
        level = level * jnp.repeat(steps, extent[axis_at] // blocks).reshape([-1 if axis == axis_at else 1 for axis in range(len(extent))])
    return level


def bell_draw(rng, extent, spread, limit, shards=(), held_as=jnp.bfloat16):
    level = block_levels(rng, extent, shards, -0.22, 0.18) if shards else 1.0
    values = jax.random.normal(rng, extent, jnp.float32) * spread * level
    return jnp.minimum(jnp.maximum(values, -limit), limit).astype(held_as)


def setup_inputs(seed: int = 0) -> dict:
    splits = jax.random.split(jax.random.key(seed), 11)
    return {
        "video": bell_draw(splits[0], (FRAMES, H, W, C), 1.0, 6.0, ((0, 4), (1, 8)), jnp.float32),
        "norm_gain": jnp.clip(1.0 + 0.18 * jax.random.normal(splits[1], (2, 2, C), jnp.float32), 0.1, 1.9),
        "space_weight": bell_draw(splits[2], (2, 3, 3, C, C), (9 * C) ** -0.5, 0.1875, (), jnp.float32),
        "time_weight": bell_draw(splits[3], (2, 3, C, C), (3 * C) ** -0.5, 0.3125, (), jnp.float32),
        "down_weight": bell_draw(splits[4], (3, 3, C, C2), (9 * C) ** -0.5, 0.1875, (), jnp.float32),
        "attn_gain": jnp.clip(1.0 + 0.18 * jax.random.normal(splits[5], (C2,), jnp.float32), 0.1, 1.9),
        "w_query": draw_w_query(jax.random.fold_in(splits[10], 71), 0),
        "w_key": draw_w_key(jax.random.fold_in(splits[10], 71), 0),
        "w_value": bell_draw(splits[8], (C2, C2), C2 ** -0.5, 0.375, (), jnp.float32),
        "w_out": bell_draw(splits[9], (C2, C2), C2 ** -0.5, 0.375, (), jnp.float32),
    }


highest = lax.Precision.HIGHEST

def norm(values, gain):
    return values * lax.rsqrt(lax.optimization_barrier(jnp.mean(values * values, -1, keepdims=True)) + 1e-06) * gain

def act(values, gain):
    return jax.nn.silu(norm(values, gain))

def conv_space(inputs, kernel):
    return lax.conv_general_dilated(inputs, kernel, (1, 1), ((1, 1), (1, 1)), dimension_numbers=('NHWC', 'HWIO', 'NHWC'), precision=highest)

def conv_time(inputs, kernel):
    padded = jnp.concatenate([inputs[:1], inputs[:1], inputs], 0)
    count = inputs.shape[0]
    total = jnp.einsum('fhwc,cd->fhwd', padded[0:count], kernel[0], precision=highest)
    total = total + jnp.einsum('fhwc,cd->fhwd', padded[1:count + 1], kernel[1], precision=highest)
    total = total + jnp.einsum('fhwc,cd->fhwd', padded[2:count + 2], kernel[2], precision=highest)
    return total

def reference(video, norm_gain, space_weight, time_weight, down_weight, attn_gain, w_query, w_key, w_value, w_out):
    state = video
    for block in range(2):
        mixed = conv_space(act(state, norm_gain[block, 0]), space_weight[block])
        state = state + conv_time(act(mixed, norm_gain[block, 1]), time_weight[block])
    lowered = lax.conv_general_dilated(state, down_weight, (2, 2), ((1, 0), (1, 0)), dimension_numbers=('NHWC', 'HWIO', 'NHWC'), precision=highest)
    flat = lowered.reshape(FRAMES, KEYS, C2)

    def attend(tokens):
        normed = norm(tokens, attn_gain)
        query = jnp.dot(normed, w_query, precision=highest) * C2 ** (-0.5)
        keys = jnp.dot(normed, w_key, precision=highest)
        values = jnp.dot(normed, w_value, precision=highest)
        scores = jnp.dot(query, keys.T, precision=highest)
        weights = jax.nn.softmax(scores, axis=-1)
        mixed = jnp.dot(weights, values, precision=highest)
        return tokens + jnp.dot(mixed, w_out, precision=highest)
    result = lax.map(attend, flat)
    blocks = result.reshape(FRAMES, N_TILE, GROUP, PT, C2).transpose(0, 2, 1, 3, 4)
    return blocks.reshape(FBLOCKS, ATOK, C2)
```

```python
import functools

import jax
import jax.numpy as jnp
from jax import lax
from jax.experimental import pallas as pl
from jax.experimental.pallas import tpu as pltpu
from jax.sharding import PartitionSpec as P

F32, BF16 = jnp.float32, jnp.bfloat16
VM = pl.BlockSpec(memory_space=pltpu.VMEM)


def call(body, outs, *args, name, flops=0):
    outs = [jax.ShapeDtypeStruct(shape, kind) for shape, kind in outs]
    moved = sum(a.size * a.dtype.itemsize for a in args) + sum(o.size * o.dtype.itemsize for o in outs)
    return pl.pallas_call(
        body,
        out_shape=outs,
        in_specs=[VM] * len(args),
        out_specs=[VM] * len(outs),
        name=name,
        compiler_params=pltpu.CompilerParams(vmem_limit_bytes=28 << 20),
        cost_estimate=pl.CostEstimate(flops=flops, bytes_accessed=moved, transcendentals=0),
    )(*args)


def halves(values):
    high = values.astype(BF16)
    return high, (values - high.astype(F32)).astype(BF16)


def left_side(values):
    high, low = halves(values)
    return jnp.concatenate([high, low, high], -1)


def right_side(values):
    high, low = halves(values)
    return jnp.concatenate([high, high, low], 0)


def mul(left, right):
    return jnp.dot(left, right, preferred_element_type=F32)


def norm(values, gain):
    return values * lax.rsqrt(jnp.mean(values * values, -1, keepdims=True) + 1e-06) * gain


def act(values, gain):
    y = norm(values, gain)
    return y / (1.0 + jnp.exp(-y))


def taps(values):
    n, w, c = values.shape
    at = lax.broadcasted_iota(jnp.int32, values.shape, 1)
    before = jnp.where(at == 0, 0.0, pltpu.roll(values, 1, 1))
    after = jnp.where(at == w - 1, 0.0, pltpu.roll(values, w - 1, 1))
    return left_side(jnp.concatenate([before, values, after], -1).reshape(n * w, 3 * c))


def pack_space(space_ref, out_ref):
    c = space_ref.shape[-1]
    for kh in range(3):
        for kw in range(3):
            high, low = halves(space_ref[kh, kw])
            cols = slice((2 - kh) * c, (3 - kh) * c)
            out_ref[kw * c : (kw + 1) * c, cols] = high
            out_ref[(3 + kw) * c : (4 + kw) * c, cols] = high
            out_ref[(6 + kw) * c : (7 + kw) * c, cols] = low


def pack_time(time_ref, out_ref):
    c = time_ref.shape[-1]
    for k in range(3):
        out_ref[:, (2 - k) * c : (3 - k) * c] = right_side(time_ref[k])


def pack_down(down_ref, out_ref):
    for kh in range(3):
        out_ref[kh] = right_side(jnp.concatenate([down_ref[kh, kw] for kw in range(3)], 0))


def pack_attn(q_ref, k_ref, v_ref, o_ref, kv_out, q_out, o_out):
    d = q_ref.shape[0]
    kv_out[:, :d] = right_side(k_ref[...])
    kv_out[:, d:] = right_side(v_ref[...])
    q_out[...] = right_side(q_ref[...])
    o_out[...] = right_side(o_ref[...])


def is_even():
    return lax.rem(lax.axis_index("tile"), 2) == 0


def conv_near(block, x_ref, near_ref, gain_ref, weight_ref, out_ref):
    n, rows, w, c = x_ref.shape
    gain = gain_ref[block, 0]
    total = [None] * rows

    def add(row, part):
        total[row] = part if total[row] is None else total[row] + part

    for row in range(rows):
        left = taps(act(x_ref[:, row], gain))
        first, last = max(row - 1, 0), min(row + 1, rows - 1)
        product = mul(left, weight_ref[:, (first - row + 1) * c : (last - row + 2) * c])
        for at in range(first, last + 1):
            add(at, product[:, (at - first) * c : (at - first + 1) * c])
    for row in range(rows):
        out_ref[:, row] = total[row].reshape(n, w, c)
    even = is_even()
    col = pl.multiple_of(jnp.where(even, 0, 2 * c), c)
    row = jnp.where(even, rows - 1, 0)
    left = taps(act(near_ref[...], gain))
    product = mul(left, weight_ref[:, pl.ds(col, c)]).reshape(n, w, c)
    out_ref[:, row] = out_ref[:, row] + product


def conv_far(block, part_ref, far_ref, gain_ref, weight_ref, out_ref):
    n, rows, w, c = part_ref.shape
    even = is_even()
    tile = lax.axis_index("tile")
    inside = jnp.logical_and(tile > 0, tile < lax.axis_size("tile") - 1)
    col = pl.multiple_of(jnp.where(even, 2 * c, 0), c)
    row = jnp.where(even, 0, rows - 1)
    far = jnp.where(inside, far_ref[...], 0.0)
    left = taps(act(far, gain_ref[block, 0]))
    product = mul(left, weight_ref[:, pl.ds(col, c)]).reshape(n, w, c)
    gain = gain_ref[block, 1]
    out_ref[...] = act(part_ref[...], gain)
    out_ref[:, row] = act(part_ref[:, row] + product, gain)


def mix_own(x_ref, u_ref, weight_ref, *out_refs):
    n, rows, w, c = x_ref.shape
    total = [x_ref[f].reshape(rows * w, c) for f in range(n)]
    for f in range(n):
        left = left_side(u_ref[f].reshape(rows * w, c))
        wide = min(3, n - f)
        product = mul(left, weight_ref[:, : wide * c])
        for k in range(wide):
            total[f + k] = total[f + k] + product[:, k * c : (k + 1) * c]
    early_ref, late_refs = out_refs[0], out_refs[1:]
    for f in range(min(n, 2)):
        early_ref[f] = total[f].reshape(rows, w, c)
    if late_refs:
        for f in range(2, n):
            late_refs[0][f - 2] = total[f].reshape(rows, w, c)
        ends(late_refs)


def ends(refs):
    if len(refs) > 1:
        x_ref, near_ref, far_ref = refs
        rows = x_ref.shape[1]
        even = is_even()
        near_ref[...] = x_ref[:, jnp.where(even, rows - 1, 0)]
        far_ref[...] = x_ref[:, jnp.where(even, 0, rows - 1)]


def mix_earlier(x_ref, u_ref, got_ref, weight_ref, *out_refs):
    n, rows, w, c = x_ref.shape
    opening = lax.axis_index("frame") == 0
    first = u_ref[0].reshape(rows * w, c)
    before = jnp.where(opening, first, got_ref[0].reshape(rows * w, c))
    last = jnp.where(opening, first, got_ref[1].reshape(rows * w, c))
    near = mul(left_side(last), weight_ref[:, c:])
    far = mul(left_side(before), weight_ref[:, 2 * c :])
    out_ref = out_refs[0]
    out_ref[0] = x_ref[0] + (near[:, :c] + far).reshape(rows, w, c)
    out_ref[1] = x_ref[1] + near[:, c:].reshape(rows, w, c)
    ends(out_refs)


def pixels(ref, n, w):
    c = ref.shape[-1]
    even = ref[pl.ds(0, n * w // 2, stride=2), :]
    odd = ref[pl.ds(1, n * w // 2, stride=2), :]
    half = w // 2
    odd3 = odd.reshape(n, half, c)
    at = lax.broadcasted_iota(jnp.int32, odd3.shape, 1)
    before = jnp.where(at == 0, 0.0, pltpu.roll(odd3, 1, 1)).reshape(n * half, c)
    return left_side(jnp.concatenate([before, even, odd], -1))


def down_own(early_ref, late_ref, weight_ref, out_ref, flat_ref):
    refs = [early_ref] + ([late_ref] if late_ref is not None else [])
    _, rows, w, c = early_ref.shape
    at = 0
    for ref in refs:
        n = ref.shape[0]
        parts = []
        for row in range(rows):
            flat_ref[: n * w] = ref[:, row].reshape(n * w, c)
            parts.append(pixels(flat_ref.at[: n * w], n, w))
        for row in range(rows // 2):
            total = mul(parts[2 * row], weight_ref[1]) + mul(parts[2 * row + 1], weight_ref[2])
            if row:
                total = total + mul(parts[2 * row - 1], weight_ref[0])
            out_ref[at : at + n, row] = total.reshape(n, w // 2, -1)
        at += n


def down_above(part_ref, above_ref, weight_ref, out_ref, flat_ref):
    n, w, c = above_ref.shape
    above = jnp.where(lax.axis_index("tile") > 0, above_ref[...], 0.0)
    flat_ref[...] = above.reshape(n * w, c)
    product = mul(pixels(flat_ref, n, w), weight_ref[0])
    out_ref[...] = part_ref[...]
    out_ref[:, 0] = part_ref[:, 0] + product.reshape(n, w // 2, -1)


def keys_values(z_ref, gain_ref, weight_ref, k_ref, v_ref):
    d = z_ref.shape[-1]
    normed = norm(z_ref[...].reshape(-1, d), gain_ref[0])
    both = mul(left_side(normed), weight_ref[...])
    high, low = halves(both[:, :d])
    k_ref[:, :d] = high
    k_ref[:, d : 2 * d] = high
    k_ref[:, 2 * d :] = low
    v_ref[...] = right_side(both[:, d:]).reshape(v_ref.shape)


def attend(query_ref, gain_ref, wq_ref, wo_ref, *refs):
    out_ref = refs[-1]
    pieces = [(refs[i], refs[i + 1]) for i in range(0, len(refs) - 1, 2)]
    d = query_ref.shape[-1]
    mine = query_ref[...]
    query = mul(left_side(norm(mine, gain_ref[0])), wq_ref[...]) * float(d) ** (-0.5)
    left = left_side(query)
    scores = [
        lax.dot_general(left, k_ref[...], (((1,), (1,)), ((), ())), preferred_element_type=F32)
        for k_ref, _ in pieces
    ]
    best = functools.reduce(jnp.maximum, [jnp.max(s, -1, keepdims=True) for s in scores])
    total, mixed = 0.0, 0.0
    for s, (_, v_ref) in zip(scores, pieces):
        weights = jnp.exp(s - best)
        total = total + jnp.sum(weights, -1, keepdims=True)
        high, low = halves(weights)
        v = v_ref[...]
        mixed = mixed + (mul(high, v[0]) + mul(low, v[1]) + mul(high, v[2]))
    mixed = mixed / total
    out_ref[...] = mine + mul(left_side(mixed), wo_ref[...])


def local(
    video,
    norm_gain,
    space_weight,
    time_weight,
    down_weight,
    attn_gain,
    w_query,
    w_key,
    w_value,
    w_out,
):
    n, rows, w, c = video.shape
    tiles, spans = lax.axis_size("tile"), lax.axis_size("frame")
    tile = lax.axis_index("tile")
    even = lax.rem(tile, 2) == 0
    outer = down_weight.shape[-1]
    late = n > 2
    pairs = [(i, i ^ 1) for i in range(tiles)]
    across = [(i, (i + 1 if i % 2 else i - 1) % tiles) for i in range(tiles)]
    onward = [(i, (i + 1) % spans) for i in range(spans)]
    below = [(i, (i + 1) % tiles) for i in range(tiles)]

    def at_row(x, row):
        return lax.dynamic_index_in_dim(x, row, 1, keepdims=False)

    def pack(body, shape, *args, name):
        return call(body, [(shape, BF16)], *args, name=name)[0]

    near_row, far_row = jnp.where(even, rows - 1, 0), jnp.where(even, 0, rows - 1)
    far = lax.ppermute(at_row(video, far_row), "tile", across)
    near = lax.ppermute(at_row(video, near_row), "tile", pairs)
    space = [pack(pack_space, (9 * c, 3 * c), space_weight[j], name=f"pack_space{j}") for j in range(2)]
    times = [pack(pack_time, (3 * c, 3 * c), time_weight[j], name=f"pack_time{j}") for j in range(2)]
    down = pack(pack_down, (3, 9 * c, outer), down_weight, name="pack_down")
    wkv, wq, wo = call(
        pack_attn,
        [((3 * outer, 2 * outer), BF16), ((3 * outer, outer), BF16), ((3 * outer, outer), BF16)],
        w_query,
        w_key,
        w_value,
        w_out,
        name="pack_attn",
    )

    def conv(block, x, near, far, tag):
        shape = x.shape
        (part,) = call(functools.partial(conv_near, block), [(shape, F32)], x, near, norm_gain, space[block], name=f"near{tag}")
        (u,) = call(functools.partial(conv_far, block), [(shape, F32)], part, far, norm_gain, space[block], name=f"far{tag}")
        return u

    def mix(block, x, u):
        got = lax.ppermute(u[n - 2 :], "frame", onward)
        size = (2, rows, w, c)
        edge = (2, w, c)
        outs = [(size, F32)]
        if late:
            outs.append(((n - 2, rows, w, c), F32))
            if block == 0:
                outs += [((n - 2, w, c), F32)] * 2
        own = call(mix_own, outs, x, u, times[block], name=f"own{block}")
        outs = [(size, F32)] + ([(edge, F32)] * 2 if block == 0 else [])
        early = call(mix_earlier, outs, own[0], u, got, times[block], name=f"earlier{block}")
        return early, own[1:]

    u = conv(0, video, near, far, "0")
    early, behind = mix(0, video, u)
    pieces = []
    for tag, group in (("1b", behind), ("1a", early)):
        if group:
            x, near, far = group
            far = lax.ppermute(far, "tile", across)
            near = lax.ppermute(near, "tile", pairs)
            pieces.append(conv(1, x, near, far, tag))
    x = jnp.concatenate([early[0]] + ([behind[0]] if late else []), 0)
    u = jnp.concatenate(pieces[::-1], 0)
    early, behind = mix(1, x, u)
    x = jnp.concatenate([early[0]] + ([behind[0]] if late else []), 0)
    above = lax.ppermute(x[:, rows - 1], "tile", below)
    zshape = (n, rows // 2, w // 2, outer)

    def own_down(x_ref, weight_ref, out_ref, flat_ref):
        down_own(x_ref, None, weight_ref, out_ref, flat_ref)

    def piece(body, args, name):
        return pl.pallas_call(
            body,
            out_shape=jax.ShapeDtypeStruct(zshape, F32),
            in_specs=[VM] * len(args),
            out_specs=VM,
            scratch_shapes=[pltpu.VMEM((n * w, c), F32)],
            name=name,
            compiler_params=pltpu.CompilerParams(vmem_limit_bytes=28 << 20),
            cost_estimate=pl.CostEstimate(flops=0, bytes_accessed=1 << 20, transcendentals=0),
        )(*args)

    z = piece(own_down, (x, down), "down_own")
    z = piece(down_above, (z, above, down), "down_above")

    group = tiles // n
    tokens = z.reshape(n, -1, outer)
    count = tokens.shape[1]
    mine = tile // group

    def frame_of(index):
        return lax.dynamic_index_in_dim(tokens, index, 0, keepdims=False)

    held = [frame_of(mine)]
    for step in range(1, n):
        pairing = [(i, i ^ (step * group)) for i in range(tiles)]
        held.append(lax.ppermute(frame_of(mine ^ step), "tile", pairing))
    gain = attn_gain.reshape(1, outer)

    def project(z, tag):
        total = z.shape[0] * z.shape[1]
        return call(
            keys_values,
            [((total, 3 * outer), BF16), ((3, total, outer), BF16)],
            z,
            gain,
            wkv,
            name=f"kv{tag}",
        )

    frame = jnp.stack(held)[:, None]
    kv = project(frame.reshape(n, count, outer), "0")
    for level in range(group.bit_length() - 1):
        pairing = [(i, i ^ (1 << level)) for i in range(tiles)]
        got = lax.ppermute(frame, "tile", pairing)
        kv += project(got.reshape(-1, count, outer), str(level + 1))
        frame = jnp.concatenate([frame, got], 1)
    frame = frame.reshape(tiles, group, count // group, outer)
    order = jnp.arange(tiles) ^ tile
    query = lax.dynamic_index_in_dim(frame, tile % group, 1, keepdims=False)[order]
    query = query.reshape(-1, outer)
    (result,) = call(attend, [(query.shape, F32)], query, gain, wq, wo, *kv, name="attend")
    return result[None]


def solution(mesh):
    in_specs = (P("frame", "tile", None, None), P(), P(), P(), P(), P(), P(), P(), P(), P())
    out_specs = P(("frame", "tile"), None, None)
    return jax.shard_map(local, mesh=mesh, in_specs=in_specs, out_specs=out_specs, check_vma=False)
```

```python
import functools

import jax
import jax.numpy as jnp
from jax import lax
from jax.experimental import pallas as pl
from jax.experimental.pallas import tpu as pltpu
from jax.sharding import PartitionSpec as P

F32, BF16 = jnp.float32, jnp.bfloat16
VM = pl.BlockSpec(memory_space=pltpu.VMEM)


def call(body, outs, *args, name, flops=0):
    outs = [jax.ShapeDtypeStruct(shape, kind) for shape, kind in outs]
    moved = sum(a.size * a.dtype.itemsize for a in args) + sum(o.size * o.dtype.itemsize for o in outs)
    return pl.pallas_call(
        body,
        out_shape=outs,
        in_specs=[VM] * len(args),
        out_specs=[VM] * len(outs),
        name=name,
        compiler_params=pltpu.CompilerParams(vmem_limit_bytes=28 << 20),
        cost_estimate=pl.CostEstimate(flops=flops, bytes_accessed=moved, transcendentals=0),
    )(*args)


def halves(values):
    high = values.astype(BF16)
    return high, (values - high.astype(F32)).astype(BF16)


def left_side(values):
    high, low = halves(values)
    return jnp.concatenate([high, low, high], -1)


def right_side(values):
    high, low = halves(values)
    return jnp.concatenate([high, high, low], 0)


def mul(left, right):
    return jnp.dot(left, right, preferred_element_type=F32)


def norm(values, gain):
    return values * lax.rsqrt(jnp.mean(values * values, -1, keepdims=True) + 1e-06) * gain


def act(values, gain):
    y = norm(values, gain)
    return y / (1.0 + jnp.exp(-y))


def taps(values):
    n, w, c = values.shape
    at = lax.broadcasted_iota(jnp.int32, values.shape, 1)
    before = jnp.where(at == 0, 0.0, pltpu.roll(values, 1, 1))
    after = jnp.where(at == w - 1, 0.0, pltpu.roll(values, w - 1, 1))
    return left_side(jnp.concatenate([before, values, after], -1).reshape(n * w, 3 * c))


def is_even():
    return lax.rem(lax.axis_index("tile"), 2) == 0


def pack_space(space_ref, out_ref):
    c = space_ref.shape[-1]
    for kh in range(3):
        at = jnp.where(is_even(), kh, 2 - kh)
        for kw in range(3):
            high, low = halves(space_ref[at, kw])
            cols = slice((2 - kh) * c, (3 - kh) * c)
            out_ref[kw * c : (kw + 1) * c, cols] = high
            out_ref[(3 + kw) * c : (4 + kw) * c, cols] = high
            out_ref[(6 + kw) * c : (7 + kw) * c, cols] = low


def pack_time(time_ref, *out_refs):
    c = time_ref.shape[-1]
    for block, out_ref in enumerate(out_refs):
        for k in range(3):
            out_ref[:, (2 - k) * c : (3 - k) * c] = right_side(time_ref[block, k])


def pack_down(down_ref, out_ref):
    for kh in range(3):
        out_ref[kh] = right_side(jnp.concatenate([down_ref[kh, kw] for kw in range(3)], 0))


def pack_attn(q_ref, k_ref, v_ref, o_ref, kv_out, q_out, o_out):
    d = q_ref.shape[0]
    kv_out[:, :d] = right_side(k_ref[...])
    kv_out[:, d:] = right_side(v_ref[...])
    q_out[...] = right_side(q_ref[...])
    o_out[...] = right_side(o_ref[...])


def conv_near(block, far_ref, near_ref, partner_ref, gain_ref, weight_ref, u_ref, part_ref):
    n, rest, w, c = near_ref.shape
    rows = rest + 1
    gain = gain_ref[block, 0]
    total = [None] * rows

    def add(row, part):
        total[row] = part if total[row] is None else total[row] + part

    for row in range(rows + 1):
        if row == rows:
            values = partner_ref[...]
        else:
            values = near_ref[:, row - 1] if row else far_ref[...]
        left = taps(act(values, gain))
        first, last = max(row - 1, 0), min(row + 1, rows - 1)
        product = mul(left, weight_ref[:, (first - row + 1) * c : (last - row + 2) * c])
        for at in range(first, last + 1):
            add(at, product[:, (at - first) * c : (at - first + 1) * c])
    part_ref[...] = total[0].reshape(n, w, c)
    for row in range(1, rows):
        u_ref[:, row - 1] = act(total[row], gain_ref[block, 1]).reshape(n, w, c)


def conv_far(block, part_ref, beyond_ref, gain_ref, weight_ref, u_ref):
    n, w, c = part_ref.shape
    tile = lax.axis_index("tile")
    inside = jnp.logical_and(tile > 0, tile < lax.axis_size("tile") - 1)
    beyond = jnp.where(inside, beyond_ref[...], 0.0)
    left = taps(act(beyond, gain_ref[block, 0]))
    product = mul(left, weight_ref[:, 2 * c :]).reshape(n, w, c)
    u_ref[...] = act(part_ref[...] + product, gain_ref[block, 1])


def mix_own(groups, x_refs, u_refs, weight_ref, out_refs):
    places = [(g, f) for g in range(groups) for f in range(x_refs[g].shape[0])]
    c = x_refs[0].shape[-1]
    shape = x_refs[0].shape[1:]
    total = [x_refs[g][f].reshape(-1, c) for g, f in places]
    for at, (g, f) in enumerate(places):
        left = left_side(u_refs[g][f].reshape(-1, c))
        wide = min(3, len(places) - at)
        product = mul(left, weight_ref[:, : wide * c])
        for k in range(wide):
            total[at + k] = total[at + k] + product[:, k * c : (k + 1) * c]
    for at, (g, f) in enumerate(places):
        out_refs[g][f] = total[at].reshape(shape)


def mix_earlier(x_ref, u_ref, got_ref, weight_ref, out_ref):
    c = x_ref.shape[-1]
    shape = x_ref.shape[1:]
    opening = lax.axis_index("frame") == 0
    first = u_ref[0].reshape(-1, c)
    before = jnp.where(opening, first, got_ref[0].reshape(-1, c))
    last = jnp.where(opening, first, got_ref[1].reshape(-1, c))
    near = mul(left_side(last), weight_ref[:, c:])
    far = mul(left_side(before), weight_ref[:, 2 * c :])
    out_ref[0] = x_ref[0] + (near[:, :c] + far).reshape(shape)
    out_ref[1] = x_ref[1] + near[:, c:].reshape(shape)


def pixels(ref, n, w):
    c = ref.shape[-1]
    half = w // 2
    even = ref[pl.ds(0, n * half, stride=2), :]
    odd = ref[pl.ds(1, n * half, stride=2), :]
    odd3 = odd.reshape(n, half, c)
    at = lax.broadcasted_iota(jnp.int32, odd3.shape, 1)
    before = jnp.where(at == 0, 0.0, pltpu.roll(odd3, 1, 1)).reshape(n * half, c)
    return left_side(jnp.concatenate([before, even, odd], -1))


def down_rows(groups, far_refs, near_refs, weight_ref, out_refs, flat_ref, held_ref):
    rows = near_refs[0].shape[1] + 1
    w, c = far_refs[0].shape[1:]
    even = is_even()

    def held(g, row):
        return near_refs[g][:, row - 1] if row else far_refs[g][...]

    start = 0
    for g in range(groups):
        n = far_refs[g].shape[0]
        parts = []
        for row in range(rows):
            values = jnp.where(even, held(g, row), held(g, rows - 1 - row))
            flat_ref[: n * w] = values.reshape(n * w, c)
            parts.append(pixels(flat_ref.at[: n * w], n, w))
        for row in range(rows // 2 + 1):
            total = None
            for kh in range(3):
                at = 2 * row - 1 + kh
                if 0 <= at < rows:
                    product = mul(parts[at], weight_ref[kh])
                    total = product if total is None else total + product
            held_ref[start : start + n, row] = total.reshape(n, w // 2, -1)
        start += n
    mine = lax.axis_index("tile") // (lax.axis_size("tile") // start)
    for step in range(start):
        out_refs[step][...] = held_ref[mine ^ step]


def attend(count, *refs):
    pieces = refs[:count]
    gain_ref, wkv_ref, wq_ref, wo_ref, out_ref, z_ref, query_ref, k_ref, v_ref = refs[count:]
    rows, w, d = pieces[0].shape
    rows -= 1
    tile = lax.axis_index("tile")
    for m in range(count):
        z_ref[tile ^ m] = pieces[m][:rows].reshape(rows * w, d)
    for m in range(count):
        at = (tile ^ m) + 1
        z_ref[at, :w] = z_ref[at, :w] + pieces[m][rows]
    gain = gain_ref[0]
    size = rows * w
    step = min(count, 8)
    for at in range(0, count, step):
        normed = norm(z_ref[at : at + step].reshape(step * size, d), gain)
        both = mul(left_side(normed), wkv_ref[...])
        tokens = slice(at * size, (at + step) * size)
        high, low = halves(both[:, :d])
        k_ref[tokens, :d] = high
        k_ref[tokens, d : 2 * d] = high
        k_ref[tokens, 2 * d :] = low
        high, low = halves(both[:, d:])
        v_ref[0, tokens] = high
        v_ref[1, tokens] = low
    part = out_ref.shape[0] // count
    for block in range(size // part):

        @pl.when(lax.rem(tile, size // part) == block)
        def _():
            for b in range(count):
                query_ref[b * part : (b + 1) * part] = z_ref[b, block * part : (block + 1) * part]

    mine = query_ref[...]
    query = mul(left_side(norm(mine, gain)), wq_ref[...]) * float(d) ** (-0.5)
    scores = lax.dot_general(
        left_side(query), k_ref[...], (((1,), (1,)), ((), ())), preferred_element_type=F32
    )
    weights = jnp.exp(scores - jnp.max(scores, -1, keepdims=True))
    total = jnp.sum(weights, -1, keepdims=True)
    high, low = halves(weights)
    mixed = mul(high, v_ref[0]) + mul(low, v_ref[0]) + mul(high, v_ref[1])
    out_ref[...] = mine + mul(left_side(mixed / total), wo_ref[...])


def local(
    video,
    norm_gain,
    space_weight,
    time_weight,
    down_weight,
    attn_gain,
    w_query,
    w_key,
    w_value,
    w_out,
):
    n, rows, w, c = video.shape
    tiles, spans = lax.axis_size("tile"), lax.axis_size("frame")
    even = lax.rem(lax.axis_index("tile"), 2) == 0
    outer = down_weight.shape[-1]
    if n == 3:
        raise ValueError("three frames")
    pairs = [(i, i ^ 1) for i in range(tiles)]
    across = [(i, (i + 1 if i % 2 else i - 1) % tiles) for i in range(tiles)]
    onward = [(i, (i + 1) % spans) for i in range(spans)]
    early, late = slice(0, 2), slice(2, n)
    ranges = [early, late] if n > 2 else [early]
    groups = len(ranges)

    def row(j):
        at = jnp.where(even, j, rows - 1 - j)
        return lax.dynamic_index_in_dim(video, at, 1, keepdims=False)

    def fold(x):
        return lax.ppermute(x, "tile", pairs)

    def cross(x):
        return lax.ppermute(x, "tile", across)

    def shift(x):
        return lax.ppermute(x[-2:], "frame", onward)

    far_all = row(0)
    near_all = jnp.stack([row(j) for j in range(1, rows)], 1)
    far = [far_all[r] for r in ranges]
    near = [near_all[r] for r in ranges]
    beyond = [None] * groups
    for g in reversed(range(groups)):
        beyond[g] = cross(far[g])
    partner_all = fold(near_all[:, -1])
    partner = [partner_all[r] for r in ranges]

    space = [
        call(pack_space, [((9 * c, 3 * c), BF16)], space_weight[j], name=f"pack_space{j}")[0] for j in range(2)
    ]
    times = call(pack_time, [((3 * c, 3 * c), BF16)] * 2, time_weight, name="pack_time")
    (down,) = call(pack_down, [((3, 9 * c, outer), BF16)], down_weight, name="pack_down")
    wkv, wq, wo = call(
        pack_attn,
        [((3 * outer, 2 * outer), BF16), ((3 * outer, outer), BF16), ((3 * outer, outer), BF16)],
        w_query,
        w_key,
        w_value,
        w_out,
        name="pack_attn",
    )

    def near_conv(block, g, far, near, partner):
        return call(
            functools.partial(conv_near, block),
            [(near.shape, F32), (far.shape, F32)],
            far,
            near,
            partner,
            norm_gain,
            space[block],
            name=f"near{block}{g}",
        )

    def far_conv(block, g, part, beyond):
        return call(
            functools.partial(conv_far, block),
            [(part.shape, F32)],
            part,
            beyond,
            norm_gain,
            space[block],
            name=f"far{block}{g}",
        )[0]

    def mix(block, x, u, tag):
        def body(*refs):
            mix_own(groups, refs[:groups], refs[groups : 2 * groups], refs[2 * groups], refs[2 * groups + 1 :])

        return call(body, [(a.shape, F32) for a in x], *x, *u, times[block], name=f"own{block}{tag}")

    def mix_in(block, x, u, got, tag):
        return call(mix_earlier, [(x.shape, F32)], x, u, got, times[block], name=f"earlier{block}{tag}")[0]

    last = groups - 1
    for block in range(2):
        u_near, part = [None] * groups, [None] * groups
        for g in reversed(range(groups)):
            u_near[g], part[g] = near_conv(block, g, far[g], near[g], partner[g])
            if g == last:
                got_near = shift(u_near[g])
        near = list(mix(block, near, u_near, "near"))
        u_far = [None] * groups
        for g in reversed(range(groups)):
            u_far[g] = far_conv(block, g, part[g], beyond[g])
            if g == last:
                got_far = shift(u_far[g])
        far = list(mix(block, far, u_far, "far"))
        if block == 0:
            partner, beyond = [None] * groups, [None] * groups
        for g in reversed(range(groups)):
            if g == 0:
                near[0] = mix_in(block, near[0], u_near[0], got_near, "near")
                far[0] = mix_in(block, far[0], u_far[0], got_far, "far")
            if block == 0:
                partner[g] = fold(near[g][:, -1])
                beyond[g] = cross(far[g])

    piece = (rows // 2 + 1, w // 2, outer)

    def down_body(*refs):
        fars, nears, refs = refs[:groups], refs[groups : 2 * groups], refs[2 * groups :]
        down_rows(groups, fars, nears, refs[0], refs[1 : 1 + n], *refs[1 + n :])

    def staged(body, outs, args, scratch, limit, name):
        return pl.pallas_call(
            body,
            out_shape=outs,
            in_specs=[VM] * len(args),
            out_specs=jax.tree.map(lambda _: VM, outs),
            scratch_shapes=[pltpu.VMEM(*s) for s in scratch],
            name=name,
            compiler_params=pltpu.CompilerParams(vmem_limit_bytes=limit << 20),
            cost_estimate=pl.CostEstimate(flops=1 << 20, bytes_accessed=1 << 20, transcendentals=0),
        )(*args)

    held = list(
        staged(
            down_body,
            [jax.ShapeDtypeStruct(piece, F32)] * n,
            (*far, *near, down),
            [((max(2, n - 2) * w, c), F32), ((n, *piece), F32)],
            28,
            "down",
        )
    )
    group = tiles // n
    held = [
        lax.ppermute(x, "tile", [(i, i ^ (step * group)) for i in range(tiles)]) if step else x
        for step, x in enumerate(held)
    ]
    pieces = {step * group: x for step, x in enumerate(held)}
    for level in range(group.bit_length() - 1):
        by = 1 << level
        pairing = [(i, i ^ by) for i in range(tiles)]
        pieces.update({m + by: lax.ppermute(x, "tile", pairing) for m, x in list(pieces.items())})
    size = (rows // 2) * (w // 2)
    total = tiles * size
    result = staged(
        functools.partial(attend, tiles),
        jax.ShapeDtypeStruct((total // group, outer), F32),
        (*[pieces[m] for m in range(tiles)], attn_gain.reshape(1, outer), wkv, wq, wo),
        [
            ((tiles + 1, size, outer), F32),
            ((total // group, outer), F32),
            ((total, 3 * outer), BF16),
            ((2, total, outer), BF16),
        ],
        28 if total < 2048 else 60,
        "attend",
    )
    return result[None]


def solution(mesh):
    in_specs = (P("frame", "tile", None, None), P(), P(), P(), P(), P(), P(), P(), P(), P())
    out_specs = P(("frame", "tile"), None, None)
    return jax.shard_map(local, mesh=mesh, in_specs=in_specs, out_specs=out_specs, check_vma=False)
```

```python
import functools

import jax
import jax.numpy as jnp
from jax import lax
from jax.experimental import pallas as pl
from jax.experimental.pallas import tpu as pltpu
from jax.sharding import PartitionSpec as P


F32, BF16 = jnp.float32, jnp.bfloat16

VM = pl.BlockSpec(memory_space=pltpu.VMEM)


def call(body, outs, *args, flops=0):
    return called(body, outs, *args, flops=flops)


def called(body, outs, *args, flops):
    outs = [jax.ShapeDtypeStruct(shape, kind) for shape, kind in outs]
    moved = sum(a.size * a.dtype.itemsize for a in args) + sum(o.size * o.dtype.itemsize for o in outs)
    return pl.pallas_call(
        body,
        out_shape=outs,
        in_specs=[VM] * len(args),
        out_specs=[VM] * len(outs),
        compiler_params=pltpu.CompilerParams(vmem_limit_bytes=28 << 20),
        cost_estimate=pl.CostEstimate(flops=flops, bytes_accessed=moved, transcendentals=0),
    )(*args)


def halves(values):
    high = values.astype(BF16)
    return high, (values - high.astype(F32)).astype(BF16)


def left_side(values):
    high, low = halves(values)
    return jnp.concatenate([high, low, high], -1)


def right_side(values):
    high, low = halves(values)
    return jnp.concatenate([high, high, low], 0)


def mul(left, right):
    return jnp.dot(left, right, preferred_element_type=F32)


def norm(values, gain):
    return values * lax.rsqrt(jnp.mean(values * values, -1, keepdims=True) + 1e-06) * gain


def act(values, gain):
    y = norm(values, gain)
    return y / (1.0 + jnp.exp(-y))


def taps(values):
    n, w, c = values.shape
    at = lax.broadcasted_iota(jnp.int32, values.shape, 1)
    before = jnp.where(at == 0, 0.0, pltpu.roll(values, 1, 1))
    after = jnp.where(at == w - 1, 0.0, pltpu.roll(values, w - 1, 1))
    return halves(jnp.concatenate([before, values, after], -1).reshape(n * w, 3 * c))


def is_even():
    return lax.rem(lax.axis_index("tile"), 2) == 0


def pack_space(space_ref, pair_ref, above_ref, below_ref):
    c = space_ref.shape[-1]
    even = is_even()
    for kh in range(3):
        at = jnp.where(even, kh, 2 - kh)
        high, low = halves(jnp.concatenate([space_ref[at, kw] for kw in range(3)], 0))
        three = jnp.concatenate([high, high, low], 0)
        for row in range(2):
            to = row + 1 - kh
            if 0 <= to < 2:
                pair_ref[row * 9 * c : (row + 1) * 9 * c, to * c : (to + 1) * c] = three
        if kh != 1:
            edge_ref = above_ref if kh == 0 else below_ref
            edge_ref[: 3 * c, :c] = high
            edge_ref[: 3 * c, c:] = low
            edge_ref[3 * c :, :c] = high
            edge_ref[3 * c :, c:] = jnp.zeros_like(low)


def pack_time(time_ref, *out_refs):
    c = time_ref.shape[-1]
    for block, out_ref in enumerate(out_refs):
        for k in range(3):
            out_ref[:, (2 - k) * c : (3 - k) * c] = right_side(time_ref[block, k])


def pack_down(down_ref, own_ref, next_ref):
    def rows(kh):
        return right_side(jnp.concatenate([down_ref[kh, kw] for kw in range(3)], 0))

    size = next_ref.shape[0]
    next_ref[...] = rows(0)
    own_ref[:size] = rows(1)
    own_ref[size:] = rows(2)


def pack_attn(q_ref, k_ref, v_ref, o_ref, qk_out, vo_out):
    d = q_ref.shape[0]
    both = lax.dot_general(
        left_side(q_ref[...] * float(d) ** (-0.5)),
        jnp.concatenate([*halves(k_ref[...])[:1] * 2, halves(k_ref[...])[1]], 1),
        (((1,), (1,)), ((), ())),
        preferred_element_type=F32,
    )
    qk_out[...] = right_side(both)
    vo_out[...] = right_side(mul(left_side(v_ref[...]), right_side(o_ref[...])))


def edge(values, weight_ref):
    n, w, c = values.shape
    both = mul(jnp.concatenate(taps(values), -1), weight_ref[...])
    return (both[:, :c] + both[:, c:]).reshape(n, w, c)


def conv_near(block, far_ref, near_ref, partner_ref, gain_ref, pair_ref, above_ref, below_ref, u_ref, part_ref):
    n, rest, w, c = near_ref.shape
    rows = rest + 1
    gain = gain_ref[block, 0]
    source = [act(near_ref[:, row - 1] if row else far_ref[...], gain) for row in range(rows)]
    total = []
    for row in range(0, rows, 2):
        left = []
        for values in source[row : row + 2]:
            high, low = taps(values)
            left += [high, low, high]
        both = mul(jnp.concatenate(left, -1), pair_ref[...])
        total += [both[:, :c].reshape(n, w, c), both[:, c:].reshape(n, w, c)]
    total[-1] = total[-1] + edge(act(partner_ref[...], gain), below_ref)
    for row in range(2, rows, 2):
        total[row] = total[row] + edge(source[row - 1], above_ref)
        total[row - 1] = total[row - 1] + edge(source[row], below_ref)
    part_ref[...] = total[0]
    for row in range(1, rows):
        u_ref[:, row - 1] = act(total[row], gain_ref[block, 1])


def conv_far(block, part_ref, beyond_ref, gain_ref, above_ref, u_ref):
    tile = lax.axis_index("tile")
    inside = jnp.logical_and(tile > 0, tile < lax.axis_size("tile") - 1)
    beyond = jnp.where(inside, beyond_ref[...], 0.0)
    product = edge(act(beyond, gain_ref[block, 0]), above_ref)
    u_ref[...] = act(part_ref[...] + product, gain_ref[block, 1])


def mix_own(groups, x_refs, u_refs, weight_ref, out_refs):
    places = [(g, f) for g in range(groups) for f in range(x_refs[g].shape[0])]
    c = x_refs[0].shape[-1]
    shape = x_refs[0].shape[1:]
    total = [x_refs[g][f].reshape(-1, c) for g, f in places]
    for at, (g, f) in enumerate(places):
        left = left_side(u_refs[g][f].reshape(-1, c))
        wide = min(3, len(places) - at)
        product = mul(left, weight_ref[:, : wide * c])
        for k in range(wide):
            total[at + k] = total[at + k] + product[:, k * c : (k + 1) * c]
    for at, (g, f) in enumerate(places):
        out_refs[g][f] = total[at].reshape(shape)


def mix_earlier(x_ref, u_ref, got_ref, weight_ref, out_ref):
    c = x_ref.shape[-1]
    shape = x_ref.shape[1:]
    opening = lax.axis_index("frame") == 0
    first = u_ref[0].reshape(-1, c)
    before = jnp.where(opening, first, got_ref[0].reshape(-1, c))
    last = jnp.where(opening, first, got_ref[1].reshape(-1, c))
    near = mul(left_side(last), weight_ref[:, c:])
    far = mul(left_side(before), weight_ref[:, 2 * c :])
    out_ref[0] = x_ref[0] + (near[:, :c] + far).reshape(shape)
    out_ref[1] = x_ref[1] + near[:, c:].reshape(shape)


def pixels(ref, n, w):
    c = ref.shape[-1]
    half = w // 2
    even = ref[pl.ds(0, n * half, stride=2), :]
    odd = ref[pl.ds(1, n * half, stride=2), :]
    odd3 = odd.reshape(n, half, c)
    at = lax.broadcasted_iota(jnp.int32, odd3.shape, 1)
    before = jnp.where(at == 0, 0.0, pltpu.roll(odd3, 1, 1)).reshape(n * half, c)
    return left_side(jnp.concatenate([before, even, odd], -1))


def down_rows(far_ref, near_ref, own_ref, next_ref, out_ref, flat_ref):
    n, rest, w, c = near_ref.shape
    rows = rest + 1
    even = is_even()

    def held(row):
        return near_ref[:, row - 1] if row else far_ref[...]

    parts = []
    for row in range(rows):
        flat_ref[: n * w] = jnp.where(even, held(row), held(rows - 1 - row)).reshape(n * w, c)
        parts.append(pixels(flat_ref.at[: n * w], n, w))
    for row in range(rows // 2 + 1):
        total = mul(parts[2 * row - 1], next_ref[...]) if row else 0.0
        if row < rows // 2:
            total = total + mul(jnp.concatenate(parts[2 * row : 2 * row + 2], -1), own_ref[...])
        out_ref[:, row] = total.reshape(n, w // 2, -1)


def spread_out(refs, out_refs):
    frames = len(out_refs)
    mine = lax.axis_index("tile") // (lax.axis_size("tile") // frames)
    start = 0
    for ref in refs:
        for f in range(ref.shape[0]):
            for step in range(frames):

                @pl.when(mine ^ step == start + f)
                def _():
                    out_refs[step][...] = ref[f]

        start += ref.shape[0]


def attend(count, *refs):
    held = refs[:count]
    gain_ref, qk_ref, vo_ref, out_ref, z_ref, query_ref, k_ref, v_ref = refs[count:]
    places = [(ref, i) for ref in held for i in range(ref.shape[0])]
    count = len(places)
    _, rows, w, d = held[0].shape
    rows -= 1
    tile = lax.axis_index("tile")
    for m, (ref, i) in enumerate(places):
        z_ref[tile ^ m] = ref[i, :rows].reshape(rows * w, d)
    for m, (ref, i) in enumerate(places):
        at = (tile ^ m) + 1
        z_ref[at, :w] = z_ref[at, :w] + ref[i, rows]
    gain = gain_ref[0]
    size = rows * w
    step = min(count, 8)
    for at in range(0, count, step):
        high, low = halves(norm(z_ref[at : at + step].reshape(step * size, d), gain))
        tokens = slice(at * size, (at + step) * size)
        k_ref[tokens, :d] = high
        k_ref[tokens, d : 2 * d] = high
        k_ref[tokens, 2 * d :] = low
        v_ref[at * size : (at + step) * size] = high
        v_ref[(count + at) * size : (count + at + step) * size] = high
        v_ref[(2 * count + at) * size : (2 * count + at + step) * size] = low
    part = out_ref.shape[0] // count
    for block in range(size // part):

        @pl.when(lax.rem(tile, size // part) == block)
        def _():
            for b in range(count):
                query_ref[b * part : (b + 1) * part] = z_ref[b, block * part : (block + 1) * part]

    mine = query_ref[...]
    query = mul(left_side(norm(mine, gain)), qk_ref[...])
    scores = lax.dot_general(
        left_side(query), k_ref[...], (((1,), (1,)), ((), ())), preferred_element_type=F32
    )
    weights = jnp.exp(scores - jnp.max(scores, -1, keepdims=True))
    total = jnp.sum(weights, -1, keepdims=True)
    mixed = mul(left_side(weights), v_ref[...])
    out_ref[...] = mine + mul(left_side(mixed / total), vo_ref[...])


def local(
    video,
    norm_gain,
    space_weight,
    time_weight,
    down_weight,
    attn_gain,
    w_query,
    w_key,
    w_value,
    w_out,
):
    n, rows, w, c = video.shape
    tiles, spans = lax.axis_size("tile"), lax.axis_size("frame")
    even = lax.rem(lax.axis_index("tile"), 2) == 0
    outer = down_weight.shape[-1]
    if n == 3:
        raise ValueError("three frames")
    pairs = [(i, i ^ 1) for i in range(tiles)]
    across = [(i, (i + 1 if i % 2 else i - 1) % tiles) for i in range(tiles)]
    onward = [(i, (i + 1) % spans) for i in range(spans)]
    early, late = slice(0, 2), slice(2, n)
    ranges = [early, late] if n > 2 else [early]
    groups = len(ranges)

    def fold(x):
        return lax.ppermute(x, "tile", pairs)

    def cross(x):
        return lax.ppermute(x, "tile", across)

    def shift(x):
        return lax.ppermute(x[-2:], "frame", onward)

    far, near, beyond = [None] * groups, [None] * groups, [None] * groups

    def load(ranges, rows_of):
        def body(video_ref, *refs):
            outs, sem = refs[:-1], refs[-1]
            even = is_even()
            copies = []
            for out, r, j in zip(outs, ranges, rows_of):
                at = jnp.where(even, j, rows - 1 - j)
                copies.append(pltpu.make_async_copy(video_ref.at[r, at], out, sem.at[len(copies)]))
                copies[-1].start()
            for copy in copies:
                copy.wait()

        outs = [jax.ShapeDtypeStruct((r.stop - r.start, w, c), F32) for r in ranges]
        return pl.pallas_call(
            body,
            out_shape=outs,
            in_specs=[pl.BlockSpec(memory_space=pl.ANY)],
            out_specs=[VM] * len(outs),
            scratch_shapes=[pltpu.SemaphoreType.DMA((len(outs),))],
            compiler_params=pltpu.CompilerParams(vmem_limit_bytes=28 << 20),
            cost_estimate=pl.CostEstimate(flops=0, bytes_accessed=1 << 18, transcendentals=0),
        )(video)

    far, beyond = [None] * groups, [None] * groups
    far[-1:] = load(ranges[-1:], [0])
    rest = load(ranges[:-1] + [slice(0, n)] * (rows - 1), [0] * (groups - 1) + list(range(1, rows)))
    far[:-1] = rest[: groups - 1]
    for g in reversed(range(groups)):
        beyond[g] = cross(far[g])
    near_all = jnp.stack(rest[groups - 1 :], 1)
    near = [near_all[r] for r in ranges]
    partner_all = fold(near_all[:, -1])
    partner = [partner_all[r] for r in ranges]

    wide = [((18 * c, 2 * c), BF16), ((6 * c, 2 * c), BF16), ((6 * c, 2 * c), BF16)]
    space = [call(pack_space, wide, space_weight[j]) for j in range(2)]
    times = call(pack_time, [((3 * c, 3 * c), BF16)] * 2, time_weight)
    down = call(pack_down, [((18 * c, outer), BF16), ((9 * c, outer), BF16)], down_weight)
    attention = call(pack_attn, [((3 * outer, outer), BF16)] * 2, w_query, w_key, w_value, w_out)

    def near_conv(block, far, near, partner):
        return call(
            functools.partial(conv_near, block),
            [(near.shape, F32), (far.shape, F32)],
            far,
            near,
            partner,
            norm_gain,
            *space[block],
        )

    def far_conv(block, part, beyond):
        return call(
            functools.partial(conv_far, block), [(part.shape, F32)], part, beyond, norm_gain, space[block][1]
        )[0]

    def mix(block, x, u):
        def body(*refs):
            mix_own(groups, refs[:groups], refs[groups : 2 * groups], refs[2 * groups], refs[2 * groups + 1 :])

        return call(body, [(a.shape, F32) for a in x], *x, *u, times[block])

    def mix_in(block, x, u, got):
        return call(mix_earlier, [(x.shape, F32)], x, u, got, times[block])[0]

    last = groups - 1
    for block in range(2):
        u_near, part = [None] * groups, [None] * groups
        for g in reversed(range(groups)):
            u_near[g], part[g] = near_conv(block, far[g], near[g], partner[g])
            if g == last:
                got_near = shift(u_near[g])
        near = list(mix(block, near, u_near))
        u_far = [None] * groups
        for g in reversed(range(groups)):
            u_far[g] = far_conv(block, part[g], beyond[g])
            if g == last:
                got_far = shift(u_far[g])
        far = list(mix(block, far, u_far))
        if block == 0:
            partner, beyond = [None] * groups, [None] * groups
        for g in reversed(range(groups)):
            if g == 0:
                near[0] = mix_in(block, near[0], u_near[0], got_near)
                far[0] = mix_in(block, far[0], u_far[0], got_far)
            if block == 0:
                partner[g] = fold(near[g][:, -1])
                beyond[g] = cross(far[g])

    piece = (rows // 2 + 1, w // 2, outer)

    def staged(body, outs, args, scratch, limit):
        return pl.pallas_call(
            body,
            out_shape=outs,
            in_specs=[VM] * len(args),
            out_specs=jax.tree.map(lambda _: VM, outs),
            scratch_shapes=[pltpu.VMEM(*s) for s in scratch],
            compiler_params=pltpu.CompilerParams(vmem_limit_bytes=limit << 20),
            cost_estimate=pl.CostEstimate(flops=1 << 20, bytes_accessed=1 << 20, transcendentals=0),
        )(*args)

    rowed = []
    for g in range(groups):
        count = far[g].shape[0]
        rowed.append(
            staged(
                down_rows,
                jax.ShapeDtypeStruct((count, *piece), F32),
                (far[g], near[g], *down),
                [((count * w, c), F32)],
                28,
            )
        )

    def spread_body(*refs):
        spread_out(refs[:groups], refs[groups:])

    held = call(spread_body, [(piece, F32)] * n, *rowed)
    group = tiles // n
    held = [
        lax.ppermute(x, "tile", [(i, i ^ (step * group)) for i in range(tiles)]) if step else x
        for step, x in enumerate(held)
    ]
    held = [x[None] for x in held]
    for level in range(group.bit_length() - 1):
        pairing = [(i, i ^ (1 << level)) for i in range(tiles)]
        got = [lax.ppermute(x, "tile", pairing) for x in held]
        if level < group.bit_length() - 2:
            held = [jnp.concatenate(both, 0) for both in zip(held, got)]
    pieces = []
    for both in zip(held, got):
        pieces += both
    size = (rows // 2) * (w // 2)
    total = tiles * size
    result = staged(
        functools.partial(attend, len(pieces)),
        jax.ShapeDtypeStruct((total // group, outer), F32),
        (*pieces, attn_gain.reshape(1, outer), *attention),
        [
            ((tiles + 1, size, outer), F32),
            ((total // group, outer), F32),
            ((total, 3 * outer), BF16),
            ((3 * total, outer), BF16),
        ],
        28 if total < 2048 else 60,
    )
    return result[None]


def solution(mesh):
    in_specs = (P("frame", "tile", None, None), P(), P(), P(), P(), P(), P(), P(), P(), P())
    out_specs = P(("frame", "tile"), None, None)
    return jax.shard_map(local, mesh=mesh, in_specs=in_specs, out_specs=out_specs, check_vma=False)
```

```python
import functools

import jax
import jax.numpy as jnp
from jax import lax
from jax.experimental import pallas as pl
from jax.experimental.pallas import tpu as pltpu
from jax.sharding import PartitionSpec as P


F32, BF16 = jnp.float32, jnp.bfloat16

VM = pl.BlockSpec(memory_space=pltpu.VMEM)


def call(body, outs, *args, flops=0):
    return called(body, outs, *args, flops=flops)


def called(body, outs, *args, flops):
    outs = [jax.ShapeDtypeStruct(shape, kind) for shape, kind in outs]
    moved = sum(a.size * a.dtype.itemsize for a in args) + sum(o.size * o.dtype.itemsize for o in outs)
    return pl.pallas_call(
        body,
        out_shape=outs,
        in_specs=[VM] * len(args),
        out_specs=[VM] * len(outs),
        compiler_params=pltpu.CompilerParams(vmem_limit_bytes=28 << 20),
        cost_estimate=pl.CostEstimate(flops=flops, bytes_accessed=moved, transcendentals=0),
    )(*args)


def halves(values):
    high = values.astype(BF16)
    return high, (values - high.astype(F32)).astype(BF16)


def left_side(values):
    high, low = halves(values)
    return jnp.concatenate([high, low, high], -1)


def right_side(values):
    high, low = halves(values)
    return jnp.concatenate([high, high, low], 0)


def mul(left, right):
    return jnp.dot(left, right, preferred_element_type=F32)


def norm(values, gain):
    return values * lax.rsqrt(jnp.mean(values * values, -1, keepdims=True) + 1e-06) * gain


def act(values, gain):
    y = norm(values, gain)
    return y / (1.0 + jnp.exp(-y))


def taps(values):
    n, w, c = values.shape
    at = lax.broadcasted_iota(jnp.int32, values.shape, 1)
    before = jnp.where(at == 0, 0.0, pltpu.roll(values, 1, 1))
    after = jnp.where(at == w - 1, 0.0, pltpu.roll(values, w - 1, 1))
    return halves(jnp.concatenate([before, values, after], -1).reshape(n * w, 3 * c))


def is_even():
    return lax.rem(lax.axis_index("tile"), 2) == 0


def pack_space(block, space_ref, pair_ref, above_ref, below_ref):
    c = space_ref.shape[-1]
    even = is_even()
    for kh in range(3):
        at = jnp.where(even, kh, 2 - kh)
        high, low = halves(jnp.concatenate([space_ref[block, at, kw] for kw in range(3)], 0))
        three = jnp.concatenate([high, high, low], 0)
        for row in range(2):
            to = row + 1 - kh
            if 0 <= to < 2:
                pair_ref[row * 9 * c : (row + 1) * 9 * c, to * c : (to + 1) * c] = three
        if kh != 1:
            edge_ref = above_ref if kh == 0 else below_ref
            edge_ref[: 3 * c, :c] = high
            edge_ref[: 3 * c, c:] = low
            edge_ref[3 * c :, :c] = high
            edge_ref[3 * c :, c:] = jnp.zeros_like(low)


def pack_time(time_ref, *out_refs):
    c = time_ref.shape[-1]
    for block, out_ref in enumerate(out_refs):
        for k in range(3):
            out_ref[:, (2 - k) * c : (3 - k) * c] = right_side(time_ref[block, k])


def pack_down(down_ref, own_ref, next_ref):
    def rows(kh):
        return right_side(jnp.concatenate([down_ref[kh, kw] for kw in range(3)], 0))

    size = next_ref.shape[0]
    next_ref[...] = rows(0)
    own_ref[:size] = rows(1)
    own_ref[size:] = rows(2)


def pack_attn(q_ref, k_ref, v_ref, o_ref, qk_out, vo_out):
    d = q_ref.shape[0]
    both = lax.dot_general(
        left_side(q_ref[...] * float(d) ** (-0.5)),
        jnp.concatenate([*halves(k_ref[...])[:1] * 2, halves(k_ref[...])[1]], 1),
        (((1,), (1,)), ((), ())),
        preferred_element_type=F32,
    )
    qk_out[...] = right_side(both)
    vo_out[...] = right_side(mul(left_side(v_ref[...]), right_side(o_ref[...])))


def edge(values, weight_ref):
    n, w, c = values.shape
    both = mul(jnp.concatenate(taps(values), -1), weight_ref[...])
    return (both[:, :c] + both[:, c:]).reshape(n, w, c)


def conv_near(block, far_ref, near_ref, partner_ref, gain_ref, pair_ref, above_ref, below_ref, u_ref, part_ref):
    n, rest, w, c = near_ref.shape
    rows = rest + 1
    gain = gain_ref[block, 0]
    source = [act(near_ref[:, row - 1] if row else far_ref[...], gain) for row in range(rows)]
    total = []
    for row in range(0, rows, 2):
        left = []
        for values in source[row : row + 2]:
            high, low = taps(values)
            left += [high, low, high]
        both = mul(jnp.concatenate(left, -1), pair_ref[...])
        total += [both[:, :c].reshape(n, w, c), both[:, c:].reshape(n, w, c)]
    total[-1] = total[-1] + edge(act(partner_ref[...], gain), below_ref)
    for row in range(2, rows, 2):
        total[row] = total[row] + edge(source[row - 1], above_ref)
        total[row - 1] = total[row - 1] + edge(source[row], below_ref)
    part_ref[...] = total[0]
    for row in range(1, rows):
        u_ref[:, row - 1] = act(total[row], gain_ref[block, 1])


def conv_far(block, part_ref, beyond_ref, gain_ref, above_ref, u_ref):
    tile = lax.axis_index("tile")
    inside = jnp.logical_and(tile > 0, tile < lax.axis_size("tile") - 1)
    beyond = jnp.where(inside, beyond_ref[...], 0.0)
    product = edge(act(beyond, gain_ref[block, 0]), above_ref)
    u_ref[...] = act(part_ref[...] + product, gain_ref[block, 1])


def mix_own(groups, x_refs, u_refs, weight_ref, out_refs):
    places = [(g, f) for g in range(groups) for f in range(x_refs[g].shape[0])]
    c = x_refs[0].shape[-1]
    shape = x_refs[0].shape[1:]
    total = [x_refs[g][f].reshape(-1, c) for g, f in places]
    for at, (g, f) in enumerate(places):
        left = left_side(u_refs[g][f].reshape(-1, c))
        wide = min(3, len(places) - at)
        product = mul(left, weight_ref[:, : wide * c])
        for k in range(wide):
            total[at + k] = total[at + k] + product[:, k * c : (k + 1) * c]
    for at, (g, f) in enumerate(places):
        out_refs[g][f] = total[at].reshape(shape)


def mix_earlier(x_ref, u_ref, got_ref, weight_ref, out_ref):
    c = x_ref.shape[-1]
    shape = x_ref.shape[1:]
    opening = lax.axis_index("frame") == 0
    first = u_ref[0].reshape(-1, c)
    before = jnp.where(opening, first, got_ref[0].reshape(-1, c))
    last = jnp.where(opening, first, got_ref[1].reshape(-1, c))
    near = mul(left_side(last), weight_ref[:, c:])
    far = mul(left_side(before), weight_ref[:, 2 * c :])
    out_ref[0] = x_ref[0] + (near[:, :c] + far).reshape(shape)
    out_ref[1] = x_ref[1] + near[:, c:].reshape(shape)


def pixels(ref, n, w):
    c = ref.shape[-1]
    half = w // 2
    even = ref[pl.ds(0, n * half, stride=2), :]
    odd = ref[pl.ds(1, n * half, stride=2), :]
    odd3 = odd.reshape(n, half, c)
    at = lax.broadcasted_iota(jnp.int32, odd3.shape, 1)
    before = jnp.where(at == 0, 0.0, pltpu.roll(odd3, 1, 1)).reshape(n * half, c)
    return left_side(jnp.concatenate([before, even, odd], -1))


def row_pixels(far_ref, near_ref, flat_ref, row):
    n, rest, w, c = near_ref.shape

    def held(row):
        return near_ref[:, row - 1] if row else far_ref[...]

    flat_ref[...] = jnp.where(is_even(), held(row), held(rest - row)).reshape(n * w, c)
    return pixels(flat_ref, n, w)


def down_next(far_ref, near_ref, next_ref, out_ref, flat_ref):
    product = mul(row_pixels(far_ref, near_ref, flat_ref, near_ref.shape[1]), next_ref[...])
    out_ref[...] = product.reshape(out_ref.shape)


def down_own(far_ref, near_ref, own_ref, next_ref, out_ref, flat_ref):
    n, rest, w, _ = near_ref.shape
    parts = [row_pixels(far_ref, near_ref, flat_ref, row) for row in range(rest + 1)]
    for row in range((rest + 1) // 2):
        total = mul(jnp.concatenate(parts[2 * row : 2 * row + 2], -1), own_ref[...])
        if row:
            total = total + mul(parts[2 * row - 1], next_ref[...])
        out_ref[:, row] = total.reshape(n, w // 2, -1)


def spread_out(groups, refs, out_refs):
    frames = len(out_refs)
    mine = lax.axis_index("tile") // (lax.axis_size("tile") // frames)
    even = is_even()
    start = 0
    for g in range(groups):
        own_ref, next_ref, got_ref = refs[g], refs[groups + g], refs[2 * groups + g]
        count, rows, w, _ = own_ref.shape
        half = w // 2
        for f in range(count):
            for step in range(frames):

                @pl.when(mine ^ step == start + f)
                def _():
                    out_ref = out_refs[step]
                    got = got_ref[f]
                    out_ref[:w] = own_ref[f, 0] + jnp.where(even, 0.0, got)
                    for row in range(1, rows):
                        out_ref[row * w : (row + 1) * w] = own_ref[f, row]
                    out_ref[rows * w :] = jnp.where(even, got[half:], next_ref[f, :half])

        start += count


def attend(count, w, *refs):
    held = refs[:count]
    gain_ref, qk_ref, vo_ref, out_ref, next_ref, z_ref, query_ref, k_ref, v_ref = refs[count:]
    places = [(ref, i) for ref in held for i in range(ref.shape[0])]
    count = len(places)
    half = w // 2
    size, d = z_ref.shape[1:]
    tile = lax.axis_index("tile")
    next_ref[0] = jnp.zeros((w, d), F32)
    for m, (ref, i) in enumerate(places):
        device = tile ^ m
        odd = lax.rem(device, 2)
        start = half * (1 - odd)
        if half % 8 == 0:
            start = pl.multiple_of(start, 8)
        next_ref[device - odd + 2, pl.ds(start, half)] = ref[i, size:]
    gain = gain_ref[0]
    for m, (ref, i) in enumerate(places):
        device = tile ^ m
        odd = lax.rem(device, 2)
        added = jnp.where(odd == 0, next_ref[device - odd], 0.0)
        z_ref[m, :w] = ref[i, :w] + added
        if size > w:
            z_ref[m, w:] = ref[i, w:size]
        high, low = halves(norm(z_ref[m], gain))
        tokens = slice(m * size, (m + 1) * size)
        k_ref[tokens, :d] = high
        k_ref[tokens, d : 2 * d] = high
        k_ref[tokens, 2 * d :] = low
        for place, values in enumerate((high, high, low)):
            at = (place * count + m) * size
            v_ref[at : at + size] = values
    part = out_ref.shape[1]
    block = lax.rem(tile, size // part)
    if part % 8 == 0:
        at = pl.multiple_of(block * part, 8)
        for m in range(count):
            query_ref[m * part : (m + 1) * part] = z_ref[m, pl.ds(at, part)]
    else:
        for b in range(size // part):

            @pl.when(block == b)
            def _():
                for m in range(count):
                    query_ref[m * part : (m + 1) * part] = z_ref[m, b * part : (b + 1) * part]

    mine = query_ref[...]
    query = mul(left_side(norm(mine, gain)), qk_ref[...])
    scores = lax.dot_general(
        left_side(query), k_ref[...], (((1,), (1,)), ((), ())), preferred_element_type=F32
    )
    weights = jnp.exp(scores - jnp.max(scores, -1, keepdims=True))
    total = jnp.sum(weights, -1, keepdims=True)
    mixed = mul(left_side(weights), v_ref[...])
    result = mine + mul(left_side(mixed / total), vo_ref[...])
    for m in range(count):
        out_ref[tile ^ m] = result[m * part : (m + 1) * part]


def local(
    video,
    norm_gain,
    space_weight,
    time_weight,
    down_weight,
    attn_gain,
    w_query,
    w_key,
    w_value,
    w_out,
):
    n, rows, w, c = video.shape
    tiles, spans = lax.axis_size("tile"), lax.axis_size("frame")
    even = lax.rem(lax.axis_index("tile"), 2) == 0
    outer = down_weight.shape[-1]
    if n == 3:
        raise ValueError("three frames")
    pairs = [(i, i ^ 1) for i in range(tiles)]
    across = [(i, (i + 1 if i % 2 else i - 1) % tiles) for i in range(tiles)]
    onward = [(i, (i + 1) % spans) for i in range(spans)]
    early, late = slice(0, 2), slice(2, n)
    ranges = [early, late] if n > 2 else [early]
    groups = len(ranges)

    def fold(x):
        return lax.ppermute(x, "tile", pairs)

    def cross(x):
        return lax.ppermute(x, "tile", across)

    def shift(x):
        return lax.ppermute(x[-2:], "frame", onward)

    far, near, beyond = [None] * groups, [None] * groups, [None] * groups

    def load(ranges, rows_of):
        def body(video_ref, *refs):
            outs, sem = refs[:-1], refs[-1]
            even = is_even()
            copies = []
            for i, (r, j, out) in enumerate(zip(ranges, rows_of, outs)):
                at = jnp.where(even, j, rows - 1 - j)
                copies.append(pltpu.make_async_copy(video_ref.at[r, at], out, sem.at[i]))
            for copy in copies:
                copy.start()
            for copy in copies:
                copy.wait()

        outs = [jax.ShapeDtypeStruct((r.stop - r.start, w, c), F32) for r in ranges]
        return pl.pallas_call(
            body,
            out_shape=outs,
            in_specs=[pl.BlockSpec(memory_space=pl.ANY)],
            out_specs=[VM] * len(outs),
            scratch_shapes=[pltpu.SemaphoreType.DMA((len(outs),))],
            compiler_params=pltpu.CompilerParams(vmem_limit_bytes=28 << 20),
            cost_estimate=pl.CostEstimate(flops=0, bytes_accessed=1 << 18, transcendentals=0),
        )(video)

    far, beyond = [None] * groups, [None] * groups
    far[-1:] = load(ranges[-1:], [0])
    rest = load(ranges[:-1] + [slice(0, n)] * (rows - 1), [0] * (groups - 1) + list(range(1, rows)))
    far[:-1] = rest[: groups - 1]
    for g in reversed(range(groups)):
        beyond[g] = cross(far[g])
    near_all = jnp.stack(rest[groups - 1 :], 1)
    near = [near_all[r] for r in ranges]
    partner_all = fold(near_all[:, -1])
    partner = [partner_all[r] for r in ranges]

    wide = [((18 * c, 2 * c), BF16), ((6 * c, 2 * c), BF16), ((6 * c, 2 * c), BF16)]
    space = [call(functools.partial(pack_space, j), wide, space_weight) for j in range(2)]
    times = call(pack_time, [((3 * c, 3 * c), BF16)] * 2, time_weight)
    down = call(pack_down, [((18 * c, outer), BF16), ((9 * c, outer), BF16)], down_weight)
    attention = call(pack_attn, [((3 * outer, outer), BF16)] * 2, w_query, w_key, w_value, w_out)

    def near_conv(block, far, near, partner):
        return call(
            functools.partial(conv_near, block),
            [(near.shape, F32), (far.shape, F32)],
            far,
            near,
            partner,
            norm_gain,
            *space[block],
        )

    def far_conv(block, part, beyond):
        return call(
            functools.partial(conv_far, block), [(part.shape, F32)], part, beyond, norm_gain, space[block][1]
        )[0]

    def mix(block, x, u):
        def body(*refs):
            mix_own(groups, refs[:groups], refs[groups : 2 * groups], refs[2 * groups], refs[2 * groups + 1 :])

        return call(body, [(a.shape, F32) for a in x], *x, *u, times[block])

    def mix_in(block, x, u, got):
        return call(mix_earlier, [(x.shape, F32)], x, u, got, times[block])[0]

    last = groups - 1
    for block in range(2):
        u_near, part = [None] * groups, [None] * groups
        for g in reversed(range(groups)):
            u_near[g], part[g] = near_conv(block, far[g], near[g], partner[g])
            if g == last:
                got_near = shift(u_near[g])
        near = list(mix(block, near, u_near))
        u_far = [None] * groups
        for g in reversed(range(groups)):
            u_far[g] = far_conv(block, part[g], beyond[g])
            if g == last:
                got_far = shift(u_far[g])
        far = list(mix(block, far, u_far))
        if block == 0:
            partner, beyond = [None] * groups, [None] * groups
        for g in reversed(range(groups)):
            if g == 0:
                near[0] = mix_in(block, near[0], u_near[0], got_near)
                far[0] = mix_in(block, far[0], u_far[0], got_far)
            if block == 0:
                partner[g] = fold(near[g][:, -1])
                beyond[g] = cross(far[g])

    half = w // 2
    piece = (rows // 2 * half + half // 2, outer)

    def staged(body, outs, args, scratch, limit):
        return pl.pallas_call(
            body,
            out_shape=outs,
            in_specs=[VM] * len(args),
            out_specs=jax.tree.map(lambda _: VM, outs),
            scratch_shapes=[pltpu.VMEM(*s) for s in scratch],
            compiler_params=pltpu.CompilerParams(vmem_limit_bytes=limit << 20),
            cost_estimate=pl.CostEstimate(flops=1 << 20, bytes_accessed=1 << 20, transcendentals=0),
        )(*args)

    own, extra, got = [None] * groups, [None] * groups, [None] * groups
    for g in reversed(range(groups)):
        count = far[g].shape[0]
        extra[g] = staged(
            down_next,
            jax.ShapeDtypeStruct((count, half, outer), F32),
            (far[g], near[g], down[1]),
            [((count * w, c), F32)],
            28,
        )
        got[g] = fold(extra[g])
        own[g] = staged(
            down_own,
            jax.ShapeDtypeStruct((count, rows // 2, half, outer), F32),
            (far[g], near[g], *down),
            [((count * w, c), F32)],
            28,
        )

    def spread_body(*refs):
        spread_out(groups, refs[: 3 * groups], refs[3 * groups :])

    held = call(spread_body, [(piece, F32)] * n, *own, *extra, *got)
    group = tiles // n
    held = [
        lax.ppermute(x, "tile", [(i, i ^ (step * group)) for i in range(tiles)]) if step else x
        for step, x in enumerate(held)
    ]
    held = [x[None] for x in held]
    for level in range(group.bit_length() - 1):
        pairing = [(i, i ^ (1 << level)) for i in range(tiles)]
        got = [lax.ppermute(x, "tile", pairing) for x in held]
        if level < group.bit_length() - 2:
            held = [jnp.concatenate(both, 0) for both in zip(held, got)]
    pieces = []
    for both in zip(held, got):
        pieces += both
    size = rows // 2 * half
    total = tiles * size
    result = staged(
        functools.partial(attend, len(pieces), half),
        jax.ShapeDtypeStruct((tiles, size // group, outer), F32),
        (*pieces, attn_gain.reshape(1, outer), *attention),
        [
            ((tiles + 2, half, outer), F32),
            ((tiles, size, outer), F32),
            ((total // group, outer), F32),
            ((total, 3 * outer), BF16),
            ((3 * total, outer), BF16),
        ],
        28 if total < 2048 else 60,
    )
    result = result.reshape(-1, outer)
    return result[None]


def solution(mesh):
    in_specs = (P("frame", "tile", None, None), P(), P(), P(), P(), P(), P(), P(), P(), P())
    out_specs = P(("frame", "tile"), None, None)
    return jax.shard_map(local, mesh=mesh, in_specs=in_specs, out_specs=out_specs, check_vma=False)
```

```python
import functools

import jax
import jax.numpy as jnp
from jax import lax
from jax.experimental import pallas as pl
from jax.experimental.pallas import tpu as pltpu
from jax.sharding import PartitionSpec as P


F32, BF16 = jnp.float32, jnp.bfloat16

VM = pl.BlockSpec(memory_space=pltpu.VMEM)


def call(body, outs, *args, flops=0):
    return called(body, outs, *args, flops=flops)


def called(body, outs, *args, flops):
    outs = [jax.ShapeDtypeStruct(shape, kind) for shape, kind in outs]
    moved = sum(a.size * a.dtype.itemsize for a in args) + sum(o.size * o.dtype.itemsize for o in outs)
    return pl.pallas_call(
        body,
        out_shape=outs,
        in_specs=[VM] * len(args),
        out_specs=[VM] * len(outs),
        compiler_params=pltpu.CompilerParams(vmem_limit_bytes=28 << 20),
        cost_estimate=pl.CostEstimate(flops=flops, bytes_accessed=moved, transcendentals=0),
    )(*args)


def halves(values):
    high = values.astype(BF16)
    return high, (values - high.astype(F32)).astype(BF16)


def left_side(values):
    high, low = halves(values)
    return jnp.concatenate([high, low, high], -1)


def right_side(values):
    high, low = halves(values)
    return jnp.concatenate([high, high, low], 0)


def mul(left, right):
    return jnp.dot(left, right, preferred_element_type=F32)


def norm(values, gain):
    return values * lax.rsqrt(jnp.mean(values * values, -1, keepdims=True) + 1e-06) * gain


def act(values, gain):
    y = norm(values, gain)
    return y / (1.0 + jnp.exp(-y))


def taps(values):
    n, w, c = values.shape
    at = lax.broadcasted_iota(jnp.int32, values.shape, 1)
    before = jnp.where(at == 0, 0.0, pltpu.roll(values, 1, 1))
    after = jnp.where(at == w - 1, 0.0, pltpu.roll(values, w - 1, 1))
    return halves(jnp.concatenate([before, values, after], -1).reshape(n * w, 3 * c))


def is_even():
    return lax.rem(lax.axis_index("tile"), 2) == 0


def pack_space(block, space_ref, pair_ref, above_ref, below_ref):
    c = space_ref.shape[-1]
    even = is_even()
    for kh in range(3):
        at = jnp.where(even, kh, 2 - kh)
        high, low = halves(jnp.concatenate([space_ref[block, at, kw] for kw in range(3)], 0))
        three = jnp.concatenate([high, high, low], 0)
        for row in range(2):
            to = row + 1 - kh
            if 0 <= to < 2:
                pair_ref[row * 9 * c : (row + 1) * 9 * c, to * c : (to + 1) * c] = three
        if kh != 1:
            edge_ref = above_ref if kh == 0 else below_ref
            edge_ref[: 3 * c, :c] = high
            edge_ref[: 3 * c, c:] = low
            edge_ref[3 * c :, :c] = high
            edge_ref[3 * c :, c:] = jnp.zeros_like(low)


def pack_time(time_ref, *out_refs):
    c = time_ref.shape[-1]
    for block, out_ref in enumerate(out_refs):
        sides = [right_side(time_ref[block, k]) for k in range(3)]
        for frame in range(4):
            for to in range(2):
                k = frame - to
                side = sides[k] if 0 <= k < 3 else jnp.zeros_like(sides[0])
                out_ref[frame * 3 * c : (frame + 1) * 3 * c, to * c : (to + 1) * c] = side


def pack_down(down_ref, own_ref, next_ref):
    def rows(kh):
        return right_side(jnp.concatenate([down_ref[kh, kw] for kw in range(3)], 0))

    size = next_ref.shape[0]
    next_ref[...] = rows(0)
    own_ref[:size] = rows(1)
    own_ref[size:] = rows(2)


def pack_attn(q_ref, k_ref, v_ref, o_ref, qk_out, vo_out):
    d = q_ref.shape[0]
    both = lax.dot_general(
        left_side(q_ref[...] * float(d) ** (-0.5)),
        jnp.concatenate([*halves(k_ref[...])[:1] * 2, halves(k_ref[...])[1]], 1),
        (((1,), (1,)), ((), ())),
        preferred_element_type=F32,
    )
    qk_out[...] = right_side(both)
    vo_out[...] = right_side(mul(left_side(v_ref[...]), right_side(o_ref[...])))


def edge(values, weight_ref):
    n, w, c = values.shape
    both = mul(jnp.concatenate(taps(values), -1), weight_ref[...])
    return (both[:, :c] + both[:, c:]).reshape(n, w, c)


def conv_near(block, far_ref, near_ref, partner_ref, gain_ref, pair_ref, above_ref, below_ref, u_ref, part_ref):
    n, rest, w, c = near_ref.shape
    rows = rest + 1
    gain = gain_ref[block, 0]
    source = [act(near_ref[:, row - 1] if row else far_ref[...], gain) for row in range(rows)]
    total = []
    for row in range(0, rows, 2):
        left = []
        for values in source[row : row + 2]:
            high, low = taps(values)
            left += [high, low, high]
        both = mul(jnp.concatenate(left, -1), pair_ref[...])
        total += [both[:, :c].reshape(n, w, c), both[:, c:].reshape(n, w, c)]
    total[-1] = total[-1] + edge(act(partner_ref[...], gain), below_ref)
    for row in range(2, rows, 2):
        total[row] = total[row] + edge(source[row - 1], above_ref)
        total[row - 1] = total[row - 1] + edge(source[row], below_ref)
    part_ref[...] = total[0]
    for row in range(1, rows):
        u_ref[:, row - 1] = act(total[row], gain_ref[block, 1])


def conv_far(block, part_ref, beyond_ref, gain_ref, above_ref, u_ref):
    tile = lax.axis_index("tile")
    inside = jnp.logical_and(tile > 0, tile < lax.axis_size("tile") - 1)
    beyond = jnp.where(inside, beyond_ref[...], 0.0)
    product = edge(act(beyond, gain_ref[block, 0]), above_ref)
    u_ref[...] = act(part_ref[...] + product, gain_ref[block, 1])


def mix_own(groups, x_refs, u_refs, weight_ref, out_refs):
    places = [(g, f) for g in range(groups) for f in range(x_refs[g].shape[0])]
    c = x_refs[0].shape[-1]
    shape = x_refs[0].shape[1:]
    left = [left_side(u_refs[g][f].reshape(-1, c)) for g, f in places]
    for at in range(0, len(places), 2):
        first = max(at - 2, 0)
        rows = slice((first - at + 2) * 3 * c, 12 * c)
        both = mul(jnp.concatenate(left[first : at + 2], -1), weight_ref[rows])
        for to in range(2):
            g, f = places[at + to]
            out_refs[g][f] = x_refs[g][f] + both[:, to * c : (to + 1) * c].reshape(shape)


def mix_earlier(x_ref, u_ref, *refs):
    c = x_ref.shape[-1]
    shape = x_ref.shape[1:]
    *got_refs, weight_ref, out_ref = refs
    frame = lax.axis_index("frame")
    left = []
    for f in range(2):
        values = got_refs[-1][f]
        if len(got_refs) > 1:
            values = jnp.where(lax.rem(frame, 2) == 1, got_refs[0][f], values)
        left.append(left_side(jnp.where(frame == 0, u_ref[0], values).reshape(-1, c)))
    both = mul(jnp.concatenate(left, -1), weight_ref[: 6 * c])
    for f in range(2):
        out_ref[f] = x_ref[f] + both[:, f * c : (f + 1) * c].reshape(shape)


def pixels(ref, n, w):
    c = ref.shape[-1]
    half = w // 2
    even = ref[pl.ds(0, n * half, stride=2), :]
    odd = ref[pl.ds(1, n * half, stride=2), :]
    odd3 = odd.reshape(n, half, c)
    at = lax.broadcasted_iota(jnp.int32, odd3.shape, 1)
    before = jnp.where(at == 0, 0.0, pltpu.roll(odd3, 1, 1)).reshape(n * half, c)
    return left_side(jnp.concatenate([before, even, odd], -1))


def row_pixels(far_ref, near_ref, flat_ref, row):
    n, rest, w, c = near_ref.shape

    def held(row):
        return near_ref[:, row - 1] if row else far_ref[...]

    flat_ref[...] = jnp.where(is_even(), held(row), held(rest - row)).reshape(n * w, c)
    return pixels(flat_ref, n, w)


def down_next(far_ref, near_ref, next_ref, out_ref, flat_ref):
    product = mul(row_pixels(far_ref, near_ref, flat_ref, near_ref.shape[1]), next_ref[...])
    out_ref[...] = product.reshape(out_ref.shape)


def down_own(far_ref, near_ref, own_ref, next_ref, out_ref, flat_ref):
    n, rest, w, _ = near_ref.shape
    parts = [row_pixels(far_ref, near_ref, flat_ref, row) for row in range(rest + 1)]
    for row in range((rest + 1) // 2):
        total = mul(jnp.concatenate(parts[2 * row : 2 * row + 2], -1), own_ref[...])
        if row:
            total = total + mul(parts[2 * row - 1], next_ref[...])
        out_ref[:, row] = total.reshape(n, w // 2, -1)


def spread_out(groups, refs, out_refs):
    frames = len(out_refs)
    mine = lax.axis_index("tile") // (lax.axis_size("tile") // frames)
    even = is_even()
    start = 0
    for g in range(groups):
        own_ref, next_ref, got_ref = refs[g], refs[groups + g], refs[2 * groups + g]
        count, rows, w, _ = own_ref.shape
        half = w // 2
        for f in range(count):
            for step in range(frames):

                @pl.when(mine ^ step == start + f)
                def _():
                    out_ref = out_refs[step]
                    got = got_ref[f]
                    out_ref[:w] = own_ref[f, 0] + jnp.where(even, 0.0, got)
                    for row in range(1, rows):
                        out_ref[row * w : (row + 1) * w] = own_ref[f, row]
                    out_ref[rows * w :] = jnp.where(even, got[half:], next_ref[f, :half])

        start += count


def attend(count, w, *refs):
    held = refs[:count]
    gain_ref, qk_ref, vo_ref, out_ref, next_ref, z_ref, query_ref, k_ref, v_ref = refs[count:]
    places = [(ref, i) for ref in held for i in range(ref.shape[0])]
    count = len(places)
    half = w // 2
    size, d = z_ref.shape[1:]
    tile = lax.axis_index("tile")
    next_ref[0] = jnp.zeros((w, d), F32)
    for m, (ref, i) in enumerate(places):
        device = tile ^ m
        odd = lax.rem(device, 2)
        start = half * (1 - odd)
        if half % 8 == 0:
            start = pl.multiple_of(start, 8)
        next_ref[device - odd + 2, pl.ds(start, half)] = ref[i, size:]
    gain = gain_ref[0]
    for m, (ref, i) in enumerate(places):
        device = tile ^ m
        odd = lax.rem(device, 2)
        added = jnp.where(odd == 0, next_ref[device - odd], 0.0)
        z = ref[i, :w] + added
        if size > w:
            z = jnp.concatenate([z, ref[i, w:size]], 0)
        z_ref[m] = z
        high, low = halves(norm(z, gain))
        tokens = slice(m * size, (m + 1) * size)
        k_ref[tokens, :d] = high
        k_ref[tokens, d : 2 * d] = high
        k_ref[tokens, 2 * d :] = low
        for place, values in enumerate((high, high, low)):
            at = (place * count + m) * size
            v_ref[at : at + size] = values
    part = out_ref.shape[1]
    block = lax.rem(tile, size // part)
    if part % 8 == 0:
        at = pl.multiple_of(block * part, 8)
        for m in range(count):
            query_ref[m * part : (m + 1) * part] = z_ref[m, pl.ds(at, part)]
    else:
        for b in range(size // part):

            @pl.when(block == b)
            def _():
                for m in range(count):
                    query_ref[m * part : (m + 1) * part] = z_ref[m, b * part : (b + 1) * part]

    mine = query_ref[...]
    query = mul(left_side(norm(mine, gain)), qk_ref[...])
    scores = lax.dot_general(
        left_side(query), k_ref[...], (((1,), (1,)), ((), ())), preferred_element_type=F32
    )
    weights = jnp.exp(scores - jnp.max(scores, -1, keepdims=True))
    total = jnp.sum(weights, -1, keepdims=True)
    mixed = mul(left_side(weights), v_ref[...])
    result = mine + mul(left_side(mixed / total), vo_ref[...])
    for m in range(count):
        out_ref[tile ^ m] = result[m * part : (m + 1) * part]


def local(
    video,
    norm_gain,
    space_weight,
    time_weight,
    down_weight,
    attn_gain,
    w_query,
    w_key,
    w_value,
    w_out,
):
    n, rows, w, c = video.shape
    tiles, spans = lax.axis_size("tile"), lax.axis_size("frame")
    even = lax.rem(lax.axis_index("tile"), 2) == 0
    outer = down_weight.shape[-1]
    if n % 2:
        raise ValueError("odd frames")
    pairs = [(i, i ^ 1) for i in range(tiles)]
    across = [(i, (i + 1 if i % 2 else i - 1) % tiles) for i in range(tiles)]
    split = ('far1',)
    onward = [(i, (i + 1) % spans) for i in range(spans)]
    early, late = slice(0, 2), slice(2, n)
    ranges = [early, late] if n > 2 else [early]
    groups = len(ranges)

    def fold(x):
        return lax.ppermute(x, "tile", pairs)

    def cross(x):
        return lax.ppermute(x, "tile", across)

    def shift(x, tag):
        x = x[-2:]
        if tag not in split:
            return [lax.ppermute(x, "frame", onward)]
        by_pair = lax.ppermute(x, "frame", [(i, i ^ 1) for i in range(spans)])
        places = []
        for i in range(spans):
            ends = i in (0, spans - 1)
            to = i if ends else (i + 1 if i % 2 else i - 1)
            places += [(t * spans + i, (t ^ ends) * spans + to) for t in range(tiles)]
        return [by_pair, lax.ppermute(x, ("tile", "frame"), places)]

    far, near, beyond = [None] * groups, [None] * groups, [None] * groups

    def load(ranges, rows_of):
        def body(video_ref, *refs):
            outs, sem = refs[:-1], refs[-1]
            even = is_even()
            copies = []
            for i, (r, j, out) in enumerate(zip(ranges, rows_of, outs)):
                at = jnp.where(even, j, rows - 1 - j)
                copies.append(pltpu.make_async_copy(video_ref.at[r, at], out, sem.at[i]))
            for copy in copies:
                copy.start()
            for copy in copies:
                copy.wait()

        outs = [jax.ShapeDtypeStruct((r.stop - r.start, w, c), F32) for r in ranges]
        return pl.pallas_call(
            body,
            out_shape=outs,
            in_specs=[pl.BlockSpec(memory_space=pl.ANY)],
            out_specs=[VM] * len(outs),
            scratch_shapes=[pltpu.SemaphoreType.DMA((len(outs),))],
            compiler_params=pltpu.CompilerParams(vmem_limit_bytes=28 << 20),
            cost_estimate=pl.CostEstimate(flops=0, bytes_accessed=1 << 18, transcendentals=0),
        )(video)

    far, beyond = [None] * groups, [None] * groups
    far[-1:] = load(ranges[-1:], [0])
    rest = load(ranges[:-1] + [slice(0, n)] * (rows - 1), [0] * (groups - 1) + list(range(1, rows)))
    far[:-1] = rest[: groups - 1]
    for g in reversed(range(groups)):
        beyond[g] = cross(far[g])
    near_all = jnp.stack(rest[groups - 1 :], 1)
    near = [near_all[r] for r in ranges]
    partner_all = fold(near_all[:, -1])
    partner = [partner_all[r] for r in ranges]

    wide = [((18 * c, 2 * c), BF16), ((6 * c, 2 * c), BF16), ((6 * c, 2 * c), BF16)]
    space = [call(functools.partial(pack_space, j), wide, space_weight) for j in range(2)]
    times = call(pack_time, [((12 * c, 2 * c), BF16)] * 2, time_weight)
    down = call(pack_down, [((18 * c, outer), BF16), ((9 * c, outer), BF16)], down_weight)
    attention = call(pack_attn, [((3 * outer, outer), BF16)] * 2, w_query, w_key, w_value, w_out)

    def near_conv(block, far, near, partner):
        return call(
            functools.partial(conv_near, block),
            [(near.shape, F32), (far.shape, F32)],
            far,
            near,
            partner,
            norm_gain,
            *space[block],
        )

    def far_conv(block, part, beyond):
        return call(
            functools.partial(conv_far, block), [(part.shape, F32)], part, beyond, norm_gain, space[block][1]
        )[0]

    def mix(block, x, u):
        def body(*refs):
            mix_own(groups, refs[:groups], refs[groups : 2 * groups], refs[2 * groups], refs[2 * groups + 1 :])

        return call(body, [(a.shape, F32) for a in x], *x, *u, times[block])

    def mix_in(block, x, u, got):
        return call(mix_earlier, [(x.shape, F32)], x, u, *got, times[block])[0]

    last = groups - 1
    for block in range(2):
        u_near, part = [None] * groups, [None] * groups
        for g in reversed(range(groups)):
            u_near[g], part[g] = near_conv(block, far[g], near[g], partner[g])
            if g == last:
                got_near = shift(u_near[g], f"near{block}")
        near = list(mix(block, near, u_near))
        u_far = [None] * groups
        for g in reversed(range(groups)):
            u_far[g] = far_conv(block, part[g], beyond[g])
            if g == last:
                got_far = shift(u_far[g], f"far{block}")
        far = list(mix(block, far, u_far))
        if block == 0:
            partner, beyond = [None] * groups, [None] * groups
        for g in reversed(range(groups)):
            if g == 0:
                near[0] = mix_in(block, near[0], u_near[0], got_near)
                far[0] = mix_in(block, far[0], u_far[0], got_far)
            if block == 0:
                partner[g] = fold(near[g][:, -1])
                beyond[g] = cross(far[g])

    half = w // 2
    piece = (rows // 2 * half + half // 2, outer)

    def staged(body, outs, args, scratch, limit):
        return pl.pallas_call(
            body,
            out_shape=outs,
            in_specs=[VM] * len(args),
            out_specs=jax.tree.map(lambda _: VM, outs),
            scratch_shapes=[pltpu.VMEM(*s) for s in scratch],
            compiler_params=pltpu.CompilerParams(vmem_limit_bytes=limit << 20),
            cost_estimate=pl.CostEstimate(flops=1 << 20, bytes_accessed=1 << 20, transcendentals=0),
        )(*args)

    own, extra, got = [None] * groups, [None] * groups, [None] * groups
    for g in reversed(range(groups)):
        count = far[g].shape[0]
        extra[g] = staged(
            down_next,
            jax.ShapeDtypeStruct((count, half, outer), F32),
            (far[g], near[g], down[1]),
            [((count * w, c), F32)],
            28,
        )
        got[g] = fold(extra[g])
        own[g] = staged(
            down_own,
            jax.ShapeDtypeStruct((count, rows // 2, half, outer), F32),
            (far[g], near[g], *down),
            [((count * w, c), F32)],
            28,
        )

    def spread_body(*refs):
        spread_out(groups, refs[: 3 * groups], refs[3 * groups :])

    held = call(spread_body, [(piece, F32)] * n, *own, *extra, *got)
    group = tiles // n
    held = [
        lax.ppermute(x, "tile", [(i, i ^ (step * group)) for i in range(tiles)]) if step else x
        for step, x in enumerate(held)
    ]
    held = [x[None] for x in held]
    for level in range(group.bit_length() - 1):
        pairing = [(i, i ^ (1 << level)) for i in range(tiles)]
        got = [lax.ppermute(x, "tile", pairing) for x in held]
        if level < group.bit_length() - 2:
            held = [jnp.concatenate(both, 0) for both in zip(held, got)]
    pieces = []
    for both in zip(held, got):
        pieces += both
    size = rows // 2 * half
    total = tiles * size
    result = staged(
        functools.partial(attend, len(pieces), half),
        jax.ShapeDtypeStruct((tiles, size // group, outer), F32),
        (*pieces, attn_gain.reshape(1, outer), *attention),
        [
            ((tiles + 2, half, outer), F32),
            ((tiles, size, outer), F32),
            ((total // group, outer), F32),
            ((total, 3 * outer), BF16),
            ((3 * total, outer), BF16),
        ],
        28 if total < 2048 else 60,
    )
    result = result.reshape(-1, outer)
    return result[None]


def solution(mesh):
    in_specs = (P("frame", "tile", None, None), P(), P(), P(), P(), P(), P(), P(), P(), P())
    out_specs = P(("frame", "tile"), None, None)
    return jax.shard_map(local, mesh=mesh, in_specs=in_specs, out_specs=out_specs, check_vma=False)
```
